32 devices in a mesh: groups: 2 (over x), ctx: 16 (over z, y, core).
Axes of the slice: x: 2, y: 2, z: 4, core: 2. Of those that a mesh axis runs over, the one named last changes fastest.
Arguments:
- queries: bfloat16 [8192, 2560], P(('groups', 'ctx')), parts along dimension 0, may hold values from -6 to 6
- keys: bfloat16 [8192, 2560], P(('groups', 'ctx')), parts along dimension 0, may hold values from -6 to 6
- values: bfloat16 [8192, 2560], P(('groups', 'ctx')), parts along dimension 0, may hold values from -6 to 6
- kv_lists: int32 [16, 4, 2, 8], P('ctx'), may hold values from 0 to 7, as said below
- kv_counts: int32 [16, 4, 2], P('ctx'), may hold values from 0 to 8, as said below
Outputs:
- attended: bfloat16 [8192, 2560], P(('groups', 'ctx')), parts along dimension 0
The draws below stay inside these ranges and needn't reach their ends.
There are 2 independent parts, one for each index of `groups`. The reference program is written for one: setup_inputs(seed, part) draws one part's arguments, and reference() takes and returns one part's arrays. A program takes and returns all parts, laid end to end along the dimension named above; an argument that names none is the same for every part. Nothing has to cross between parts.
Inputs may be any that keep to these rules, and one draw needn't show every extreme that they name: For every device d, level k and side s, the first 8 // 2**k entries of kv_lists[d, k, s] are distinct block indices; later entries are never read. kv_counts[d, k, s] is at most 8 // 2**k and reaches it for some device at every level and side; it is 0 exactly where the partner d - 2**k (s = 0) or d + 2**k (s = 1) lies outside 0 to 15, else 1 or more.
All inputs are finite; a program needn't handle non-finite values.
Results may differ from the reference program's by a relative error of at most 0.005.
Values may be sent and summed in bfloat16 or wider, within the bound.
A program may use at most 128 MiB of HBM per device.

```python
import math
import jax
import jax.numpy as jnp
from jax import lax

HEADS = 20
HEAD = 128
ROWS = 256
NBLK = 8
LEVELS = 4
BS = 32
TOKENS = 4096
N_CTX = 16


def draw_queries(key, part):
    base_rows = jax.random.normal(jax.random.fold_in(key, 1), (TOKENS, HEADS * HEAD), jnp.float32) * 1.8
    return jnp.clip(base_rows, -6.0, 6.0).astype(jnp.bfloat16)


def draw_keys(key, part):
    base_rows = jax.random.normal(jax.random.fold_in(key, 2), (TOKENS, HEADS * HEAD), jnp.float32)
    return jnp.clip(base_rows, -6.0, 6.0).astype(jnp.bfloat16)


def draw_kv_lists(key, part):
    random_keys = jax.random.randint(jax.random.fold_in(key, 21), (N_CTX, LEVELS, 2, NBLK), 0, 1 << 20)
    random_keys = random_keys * NBLK + jnp.arange(NBLK, dtype=jnp.int32)
    return jnp.argsort(random_keys, axis=-1).astype(jnp.int32)


def draw_kv_counts(key, part):
    device_ids = jnp.arange(N_CTX, dtype=jnp.int32)[:, None, None]
    level_ids = jnp.arange(LEVELS, dtype=jnp.int32)[None, :, None]
    side_ids = jnp.arange(2, dtype=jnp.int32)[None, None, :]
    distance = jnp.left_shift(jnp.int32(1), level_ids)
    partner = jnp.where(side_ids == 0, device_ids - distance, device_ids + distance)
    present = (partner >= 0) & (partner < N_CTX)
    capacity = NBLK // distance
    random_pick = jax.random.randint(jax.random.fold_in(key, 22), (N_CTX, LEVELS, 2), 0, 1 << 20) % capacity + 1
    saturated = device_ids % 4 == 0
    counted = jnp.where(present, jnp.where(saturated, capacity, random_pick), 0)
    return counted.astype(jnp.int32)


def shard_levels(rng, shape, shards, low, top_value):
    def one(position, parts):
        steps = jax.random.uniform(jax.random.fold_in(jax.random.fold_in(rng, 6), position), (parts,), jnp.float32, low / len(shards), top_value / len(shards))
        return jnp.repeat(jnp.exp(steps), shape[position] // parts).reshape((-1,) + (1,) * (len(shape) - position - 1))

    level = one(*shards[0])
    for cut in shards[1:]:
        level = level * one(*cut)
    return level


def noise(own_key, extent, deviation, limit, split=(), kind=jnp.bfloat16):
    values = deviation * jax.random.normal(own_key, extent, jnp.float32)
    if split:
        values = values * shard_levels(own_key, extent, split, -0.22, 0.18)
    return jnp.clip(values, -limit, limit).astype(kind)


def setup_inputs(seed: int = 0, part: int = 0) -> dict:
    streams_of = jax.random.split(jax.random.key(seed), 6)
    part_splits = jax.random.split(jax.random.fold_in(streams_of[5], part), 6)
    return {
        "queries": draw_queries(jax.random.fold_in(jax.random.fold_in(streams_of[5], part), 71), part),
        "keys": draw_keys(jax.random.fold_in(jax.random.fold_in(streams_of[5], part), 71), part),
        "values": noise(part_splits[2], (TOKENS, HEADS * HEAD), 1.0, 6.0, ((0, 16),)),
        "kv_lists": draw_kv_lists(jax.random.fold_in(streams_of[5], 71), part),
        "kv_counts": draw_kv_counts(jax.random.fold_in(streams_of[5], 71), part),
    }


def reference(queries, keys, values, kv_lists, kv_counts):
    width = HEADS * HEAD
    key_blocks = keys.reshape(N_CTX, NBLK, BS, width)
    value_blocks = values.reshape(N_CTX, NBLK, BS, width)

    def one_device(device_id):
        query_rows = lax.dynamic_slice_in_dim(queries, device_id * ROWS, ROWS, 0)
        key_parts = [key_blocks[device_id].reshape(ROWS, width)]
        value_parts = [value_blocks[device_id].reshape(ROWS, width)]
        flag_parts = [jnp.ones((ROWS,), dtype=bool)]
        for level_id in range(LEVELS):
            distance = 2 ** level_id
            capacity = NBLK // distance
            for side_id in range(2):
                partner = device_id - distance if side_id == 0 else device_id + distance
                safe_partner = jnp.clip(partner, 0, N_CTX - 1).astype(jnp.int32)
                chosen = kv_lists[device_id, level_id, side_id, :capacity].astype(jnp.int32)
                counted = kv_counts[device_id, level_id, side_id]
                key_parts.append(key_blocks[safe_partner][chosen].reshape(capacity * BS, width))
                value_parts.append(value_blocks[safe_partner][chosen].reshape(capacity * BS, width))
                slot_ids = jnp.arange(capacity * BS, dtype=jnp.int32) // BS
                flag_parts.append(slot_ids < counted)
        all_keys = jnp.concatenate(key_parts, axis=0).astype(jnp.float32)
        all_values = jnp.concatenate(value_parts, axis=0).astype(jnp.float32)
        allowed = jnp.concatenate(flag_parts, axis=0)
        query_heads = query_rows.astype(jnp.float32).reshape(ROWS, HEADS, HEAD)
        key_heads = all_keys.reshape(-1, HEADS, HEAD)
        value_heads = all_values.reshape(-1, HEADS, HEAD)
        scores = jnp.einsum('qhd,khd->hqk', query_heads, key_heads) * (1.0 / math.sqrt(HEAD))
        scores = jnp.where(allowed[None, None, :], scores, -1e+30)
        top_score = lax.optimization_barrier(jnp.max(scores, axis=-1, keepdims=True))
        weights = jnp.exp(scores - top_score)
        weight_total = lax.optimization_barrier(jnp.sum(weights, axis=-1))
        rounded = lax.optimization_barrier(weights.astype(jnp.bfloat16)).astype(jnp.float32)
        mixed_values = jnp.einsum('hqk,khd->qhd', rounded, value_heads)
        result = mixed_values / jnp.transpose(weight_total)[:, :, None]
        return result.reshape(ROWS, width).astype(jnp.bfloat16)
    results = lax.map(one_device, jnp.arange(N_CTX, dtype=jnp.int32))
    return results.reshape(TOKENS, width)
```

```python
import functools
import math

import jax
import jax.numpy as jnp
from jax import lax
from jax.experimental import pallas as pl
from jax.experimental.pallas import tpu as pltpu
from jax.sharding import PartitionSpec as P

HEAD = 128
MASKED = -1e30
CHUNKS = 4
MESH = pl.DeviceIdType.MESH


def body(
    n_ctx, nblk,
    q_ref, k_ref, v_ref, pick_near, pick_far, bias_ref, out_ref,
    near, forwarded, big, inner, outer, far, far_pack, relay_pack, got_near, got_far,
    acc, top, tot,
    s_list, s_near, s_full, s_far, s_relay, s_fwd, s_pack,
    r_list, r_near, r_big, r_far, r_fwd, r_outer,
):
    rows, width = q_ref.shape
    heads = width // HEAD
    bs = rows // nblk
    half = rows // 2
    cap1, cap2, cap3 = nblk // 2, nblk // 4, nblk // 8
    rate = math.log2(math.e) / math.sqrt(HEAD)

    d = lax.axis_index("ctx")
    place = lax.rem(d, 4)
    quad = d // 4
    quads = n_ctx // 4
    left = place < 2
    s = jnp.where(left, 1, -1)
    gate = (place == 1) | (place == 2)
    outermost = jnp.logical_not(gate)
    has_out = jnp.where(left, quad > 0, quad < quads - 1)
    has_in = jnp.where(left, quad < quads - 1, quad > 0)
    side_in = jnp.where(left, 1, 0)
    side_out = 1 - side_in
    twin = jnp.where(gate, d - s, d + s)
    relay_to = d + 3 * s
    relay_from = d - 3 * s
    relays = gate & has_in
    gets_relay = outermost & has_out
    forwards = gate | has_out
    fwd_arrives = outermost | has_out
    full_to = jnp.where(gate, d + s, d + 2 * s)
    full_slot = jnp.where(gate, 0, 1)

    fars = []
    for distance in (4, 8):
        fars.append((d + distance, d + distance < n_ctx))
        fars.append((d - distance, d - distance >= 0))

    def to(device):
        return {"ctx": device}

    barrier = pltpu.get_barrier_semaphore()
    partners = [(p, ok) for p, ok in fars]
    always = jnp.bool_(True)
    partners += [
        (twin, always),
        (d + 2 * s, always),
        (d + s, gate),
        (relay_to, relays),
        (relay_from, gets_relay),
    ]
    count = jnp.int32(0)
    for p, ok in partners:
        count = count + ok.astype(jnp.int32)

        @pl.when(ok)
        def _(p=p):
            pl.semaphore_signal(barrier, inc=1, device_id=to(p), device_id_type=MESH)

    pl.semaphore_wait(barrier, count)

    def remote(src, dst, ssem, rsem, device):
        return pltpu.make_async_remote_copy(
            src_ref=src, dst_ref=dst, send_sem=ssem, recv_sem=rsem,
            device_id=to(device), device_id_type=MESH,
        )

    far_rows = (cap2 * bs, cap2 * bs, cap3 * bs, cap3 * bs)
    far_start = (0, cap2 * bs, 2 * cap2 * bs, (2 * cap2 + cap3) * bs)

    def pick_copy(i, device):
        if i == 4:
            return remote(pick_near.at[side_out], got_near, s_list.at[4], r_list.at[4], device)
        r = pl.ds(far_start[i], far_rows[i])
        return remote(pick_far.at[r], got_far.at[r], s_list.at[i], r_list.at[i], device)

    flip = (1, 0, 3, 2)
    sends_list = [(flip[i], p, ok) for i, (p, ok) in enumerate(fars)] + [(4, relay_from, gets_relay)]
    has_list = [(i, p, ok) for i, (p, ok) in enumerate(fars)] + [(4, relay_to, relays)]

    step_cols = 4 * HEAD if width % (4 * HEAD) == 0 else HEAD

    def gather(pick, sources, dst_of):
        def go(i, carry):
            cols = pl.ds(pl.multiple_of(i * step_cols, step_cols), step_cols)
            for kv in range(2):
                rows_got = jnp.dot(pick, sources[kv](cols), preferred_element_type=jnp.float32)
                dst_of(kv, cols, rows_got.astype(jnp.bfloat16))
            return carry

        lax.fori_loop(0, width // step_cols, go, 0)

    def near_copy(c):
        return remote((k_ref, v_ref)[c], near.at[c], s_near.at[c], r_near.at[c], twin)

    def part(c):
        return c // 2, pl.ds((c % 2) * half, half)

    def full_copy(c):
        kv, r = part(c)
        return remote(
            (k_ref, v_ref)[kv].at[r], big.at[full_slot, kv, r],
            s_full.at[c], r_big.at[full_slot, c], full_to,
        )

    def relay_copy(c):
        kv, r = part(c)
        return remote(big.at[1, kv, r], big.at[0, kv, r], s_relay.at[c], r_big.at[0, c], relay_to)

    def fwd_copy(c):
        kv, r = part(c)
        return remote(big.at[0, kv, r], forwarded.at[kv, r], s_fwd.at[c], r_fwd.at[c], twin)

    def big_wait(slot, c):
        kv, r = part(c)
        remote(big.at[slot, kv, r], big.at[slot, kv, r], s_relay.at[c], r_big.at[slot, c], twin).wait_recv()

    def far_copy(i):
        r = pl.ds(far_start[i], far_rows[i])
        return remote(far_pack.at[:, r], far.at[:, r], s_far.at[i], r_far.at[i], fars[i][0])

    def pack_copy():
        return remote(relay_pack, outer, s_pack, r_outer, relay_to)

    for slot, p, ok in sends_list:
        @pl.when(ok)
        def _(slot=slot, p=p):
            pick_copy(slot, p).start()

    for c in range(CHUNKS):
        full_copy(c).start()
    for c in range(2):
        near_copy(c).start()

    for slot, p, ok in has_list:
        @pl.when(ok)
        def _(slot=slot, p=p):
            pick_copy(slot, p).wait_recv()
            if slot < 4:
                r = pl.ds(far_start[slot], far_rows[slot])

                def put(kv, cols, x):
                    far_pack[kv, r, cols] = x

                gather(got_far[r, :], (lambda c: k_ref[:, c], lambda c: v_ref[:, c]), put)
                far_copy(slot).start()

    def full_bias(side):
        return bias_ref[side]

    def listed_bias(side):
        return bias_ref[2 + side, :, pl.ds(0, cap1 * bs)]

    def wide(x, n):
        k = n // HEAD
        whole = jnp.concatenate([x] * k, axis=1) if k > 1 else x
        if n % HEAD:
            whole = jnp.concatenate([x] * (k + 1), axis=1)[:, :n]
        return whole

    def folded(p):
        n = p.shape[1]
        total = p[:, :HEAD]
        for i in range(1, n // HEAD):
            total = total + p[:, i * HEAD:(i + 1) * HEAD]
        return total

    def attend(keys, values, bias, first=False):
        def one(h):
            cols = pl.ds(pl.multiple_of(h * HEAD, HEAD), HEAD)
            sc = lax.dot_general(
                q_ref[:, cols], keys(cols), (((1,), (1,)), ((), ())),
                preferred_element_type=jnp.float32,
            ) * rate
            if bias is not None:
                sc = sc + bias
            n = sc.shape[1]
            best = jnp.broadcast_to(jnp.max(sc, axis=1, keepdims=True), (rows, HEAD))
            if not first:
                old = top[h]
                best = jnp.maximum(old, best)
            p = jnp.exp2(sc - wide(best, n))
            mixed = jnp.dot(
                p.astype(jnp.bfloat16), values(cols), preferred_element_type=jnp.float32
            )
            part_sum = folded(p)
            if first:
                tot[h] = part_sum
                acc[h] = mixed
            else:
                factor = jnp.exp2(old - best)
                tot[h] = tot[h] * factor + part_sum
                acc[h] = acc[h] * factor + mixed
            top[h] = best

        def step(i, carry):
            one(2 * i)
            one(2 * i + 1)
            return carry

        if heads % 2:
            lax.fori_loop(0, heads, lambda i, c: (one(i), c)[1], 0)
        else:
            lax.fori_loop(0, heads // 2, step, 0)

    def put_inner(kv, cols, x):
        inner[kv, :, cols] = x

    def put_outer(kv, cols, x):
        outer[kv, :, cols] = x

    attend(lambda c: k_ref[:, c], lambda c: v_ref[:, c], None, first=True)

    for c in range(2):
        near_copy(c).wait_recv()
    attend(
        lambda c: near[0, :, c], lambda c: near[1, :, c],
        full_bias(jnp.where(gate, side_out, side_in)),
    )

    @pl.when(gate)
    def _():
        for c in range(2):
            big_wait(1, c)

            @pl.when(has_in)
            def _(c=c):
                relay_copy(c).start()

            big_wait(0, c)
            fwd_copy(c).start()

    arrives = [fars[1], fars[0], fars[3], fars[2]]
    for i in range(4):
        @pl.when(arrives[i][1])
        def _(i=i):
            far_copy(i).wait_recv()

        @pl.when(jnp.logical_not(arrives[i][1]))
        def _(i=i):
            for kv in range(2):
                far[kv, pl.ds(far_start[i], far_rows[i]), :] = jnp.zeros(
                    (far_rows[i], width), far.dtype
                )

    spare = (-sum(far_rows)) % HEAD
    if spare:
        for kv in range(2):
            far[kv, pl.ds(sum(far_rows), spare), :] = jnp.zeros((spare, width), far.dtype)
    far_bias = bias_ref[4, :, pl.ds(0, sum(far_rows) + spare)]
    attend(lambda c: far[0, :, c], lambda c: far[1, :, c], far_bias)

    @pl.when(gate)
    def _():
        for c in range(2, CHUNKS):
            big_wait(1, c)

            @pl.when(has_in)
            def _(c=c):
                relay_copy(c).start()

            big_wait(0, c)
            fwd_copy(c).start()

        @pl.when(has_in)
        def _():
            def put_relay(kv, cols, x):
                relay_pack[kv, :, cols] = x

            gather(got_near[...], (lambda c: big[0, 0, :, c], lambda c: big[0, 1, :, c]), put_relay)
            pack_copy().start()

        gather(pick_near[side_in], (lambda c: big[1, 0, :, c], lambda c: big[1, 1, :, c]), put_inner)

    @pl.when(gets_relay)
    def _():
        for c in range(CHUNKS):
            big_wait(0, c)
            fwd_copy(c).start()

    @pl.when(outermost)
    def _():
        for c in range(CHUNKS):
            fwd_copy(c).wait_recv()
        gather(pick_near[side_in], (lambda c: forwarded[0, :, c], lambda c: forwarded[1, :, c]), put_inner)

    attend(lambda c: inner[0, :, c], lambda c: inner[1, :, c], listed_bias(side_in))

    @pl.when(forwards)
    def _():
        attend(
            lambda c: big[0, 0, :, c], lambda c: big[0, 1, :, c],
            full_bias(jnp.where(gate, side_in, side_out)),
        )

    @pl.when(gate & has_out)
    def _():
        for c in range(CHUNKS):
            fwd_copy(c).wait_recv()
        gather(pick_near[side_out], (lambda c: forwarded[0, :, c], lambda c: forwarded[1, :, c]), put_outer)

    @pl.when(gets_relay)
    def _():
        pack_copy().wait_recv()

    @pl.when(has_out)
    def _():
        attend(lambda c: outer[0, :, c], lambda c: outer[1, :, c], listed_bias(side_out))

    def finish(h, carry):
        cols = pl.ds(pl.multiple_of(h * HEAD, HEAD), HEAD)
        total = jnp.sum(tot[h], axis=1, keepdims=True)
        out_ref[:, cols] = (acc[h] / total).astype(out_ref.dtype)
        return carry

    lax.fori_loop(0, heads, finish, 0)

    for slot, p, ok in sends_list:
        @pl.when(ok)
        def _(slot=slot, p=p):
            pick_copy(slot, p).wait_send()
    for c in range(CHUNKS):
        full_copy(c).wait_send()
    for c in range(2):
        near_copy(c).wait_send()
    for i, (p, ok) in enumerate(fars):
        @pl.when(ok)
        def _(i=i):
            far_copy(i).wait_send()

    @pl.when(relays)
    def _():
        for c in range(CHUNKS):
            relay_copy(c).wait_send()
        pack_copy().wait_send()

    @pl.when(forwards)
    def _():
        for c in range(CHUNKS):
            fwd_copy(c).wait_send()


def shards(n_ctx, queries, keys, values, kv_lists, kv_counts):
    rows, width = queries.shape
    heads = width // HEAD
    nblk = kv_lists.shape[3]
    levels = kv_lists.shape[1]
    bs = rows // nblk
    counts = kv_counts[0]
    block = jnp.arange(rows, dtype=jnp.int32) // bs
    slot = jnp.arange(nblk, dtype=jnp.int32)
    named = kv_lists[0, 0][:, :, None] == block[None, None, :]
    used = slot[None, :, None] < counts[0][:, None, None]
    full = jnp.any(named & used, axis=1)
    listed = block[None, :] < counts[1][:, None]
    start, far_seen = 0, jnp.zeros((rows,), jnp.bool_)
    for level in (2, 3):
        for side in range(2):
            at = block - start
            far_seen = far_seen | ((at >= 0) & (at < counts[level, side]))
            start += nblk >> level
    seen = jnp.concatenate([full, listed, far_seen[None], jnp.zeros((3, rows), jnp.bool_)], axis=0)
    row = jnp.arange(rows, dtype=jnp.int32)

    def picks(level):
        cap = nblk >> level
        wanted = kv_lists[0, level, :, :cap, None] * bs + jnp.arange(bs, dtype=jnp.int32)
        wanted = wanted.reshape(2, cap * bs, 1)
        return (wanted == row).astype(jnp.bfloat16)

    pick_near = picks(1)
    pick_far = jnp.concatenate([picks(2).reshape(-1, rows), picks(3).reshape(-1, rows)], axis=0)
    bias = jnp.where(seen, 0.0, MASKED).astype(jnp.float32)[:, None, :]
    cap1 = nblk // 2
    far_rows = 2 * (nblk // 4 + nblk // 8) * bs
    far_room = far_rows + (-far_rows) % HEAD
    kv = jnp.bfloat16
    vmem = pl.BlockSpec(memory_space=pltpu.VMEM)
    dma = pltpu.SemaphoreType.DMA
    return pl.pallas_call(
        functools.partial(body, n_ctx, nblk),
        out_shape=jax.ShapeDtypeStruct((rows, width), jnp.bfloat16),
        in_specs=[vmem] * 6,
        out_specs=vmem,
        scratch_shapes=[
            pltpu.VMEM((2, rows, width), kv),
            pltpu.VMEM((2, rows, width), kv),
            pltpu.VMEM((2, 2, rows, width), kv),
            pltpu.VMEM((2, cap1 * bs, width), kv),
            pltpu.VMEM((2, cap1 * bs, width), kv),
            pltpu.VMEM((2, far_room, width), kv),
            pltpu.VMEM((2, far_rows, width), kv),
            pltpu.VMEM((2, cap1 * bs, width), kv),
            pltpu.VMEM((cap1 * bs, rows), kv),
            pltpu.VMEM((far_rows, rows), kv),
            pltpu.VMEM((heads, rows, HEAD), jnp.float32),
            pltpu.VMEM((heads, rows, HEAD), jnp.float32),
            pltpu.VMEM((heads, rows, HEAD), jnp.float32),
            dma((5,)), dma((2,)), dma((CHUNKS,)), dma((4,)), dma((CHUNKS,)), dma((CHUNKS,)), dma,
            dma((5,)), dma((2,)), dma((2, CHUNKS)), dma((4,)), dma((CHUNKS,)), dma,
        ],
        compiler_params=pltpu.CompilerParams(
            collective_id=0, has_side_effects=True, vmem_limit_bytes=60 * 1024 * 1024
        ),
        name="radial",
    )(queries, keys, values, pick_near, pick_far, bias)


def solution(mesh):
    in_specs = (
        P(("groups", "ctx"), None),
        P(("groups", "ctx"), None),
        P(("groups", "ctx"), None),
        P("ctx", None, None, None),
        P("ctx", None, None),
    )
    out_specs = P(("groups", "ctx"), None)
    return jax.shard_map(
        functools.partial(shards, mesh.shape["ctx"]),
        mesh=mesh, in_specs=in_specs, out_specs=out_specs, check_vma=False,
    )
```

```python
import functools
import math

import jax
import jax.numpy as jnp
from jax import lax
from jax.experimental import pallas as pl
from jax.experimental.pallas import tpu as pltpu
from jax.sharding import PartitionSpec as P

HEAD = 128
MASKED = -1e30
CHUNKS = 4
MESH = pl.DeviceIdType.MESH


def body(
    n_ctx, nblk,
    q_ref, k_ref, v_ref, lists, counts, out_ref,
    near, forwarded, big, inner, outer, far, far_pack, relay_pack, hop, pick_near, pick_far, got_near, got_far,
    acc, top, tot,
    s_list, s_near, s_full, s_far, s_relay, s_fwd, s_pack, s_hop,
    r_list, r_near, r_big, r_far, r_fwd, r_outer, r_hop,
):
    rows, width = q_ref.shape
    heads = width // HEAD
    bs = rows // nblk
    half = rows // 2
    cap1, cap2, cap3 = nblk // 2, nblk // 4, nblk // 8
    rate = math.log2(math.e) / math.sqrt(HEAD)

    d = lax.axis_index("ctx")
    place = lax.rem(d, 4)
    quad = d // 4
    quads = n_ctx // 4
    left = place < 2
    s = jnp.where(left, 1, -1)
    gate = (place == 1) | (place == 2)
    outermost = jnp.logical_not(gate)
    has_out = jnp.where(left, quad > 0, quad < quads - 1)
    has_in = jnp.where(left, quad < quads - 1, quad > 0)
    side_in = jnp.where(left, 1, 0)
    side_out = 1 - side_in
    twin = jnp.where(gate, d - s, d + s)
    relay_to = d + 3 * s
    relay_from = d - 3 * s
    relays = gate & has_in
    gets_relay = outermost & has_out
    forwards = gate | has_out
    fwd_arrives = outermost | has_out

    fars = []
    for distance in (4, 8):
        fars.append((d + distance, d + distance < n_ctx))
        fars.append((d - distance, d - distance >= 0))

    far_rows = (cap2 * bs, cap2 * bs, cap3 * bs, cap3 * bs)
    far_start = (0, cap2 * bs, 2 * cap2 * bs, (2 * cap2 + cap3) * bs)
    ahead = lax.broadcasted_iota(jnp.int32, (bs, rows), 1) - lax.broadcasted_iota(
        jnp.int32, (bs, rows), 0
    )

    def single_ones(level, side, j):
        hit = ahead == lists[0, level, side, j] * bs
        return jnp.where(hit, 1.0, 0.0).astype(jnp.bfloat16)

    for i in range(4):
        for j in range(far_rows[i] // bs):
            pick_far[pl.ds(far_start[i] + j * bs, bs), :] = single_ones(2 + i // 2, i % 2, j)
    for side in range(2):
        for j in range(cap1):
            pick_near[side, pl.ds(j * bs, bs), :] = single_ones(1, side, j)

    def to(device):
        return {"ctx": device}

    barrier = pltpu.get_barrier_semaphore()
    partners = [(p, ok) for p, ok in fars]
    always = jnp.bool_(True)
    partners += [
        (twin, always),
        (d + s, gate),
        (d + 3 * s, outermost),
        (relay_to, relays),
        (relay_from, gets_relay),
    ]
    count = jnp.int32(0)
    for p, ok in partners:
        count = count + ok.astype(jnp.int32)

        @pl.when(ok)
        def _(p=p):
            pl.semaphore_signal(barrier, inc=1, device_id=to(p), device_id_type=MESH)

    pl.semaphore_wait(barrier, count)

    def remote(src, dst, ssem, rsem, device):
        return pltpu.make_async_remote_copy(
            src_ref=src, dst_ref=dst, send_sem=ssem, recv_sem=rsem,
            device_id=to(device), device_id_type=MESH,
        )

    def pick_copy(i, device):
        if i == 4:
            return remote(pick_near.at[side_out], got_near, s_list.at[4], r_list.at[4], device)
        r = pl.ds(far_start[i], far_rows[i])
        return remote(pick_far.at[r], got_far.at[r], s_list.at[i], r_list.at[i], device)

    flip = (1, 0, 3, 2)
    sends_list = [(flip[i], p, ok) for i, (p, ok) in enumerate(fars)] + [(4, relay_from, gets_relay)]
    has_list = [(i, p, ok) for i, (p, ok) in enumerate(fars)] + [(4, relay_to, relays)]

    step_cols = 4 * HEAD if width % (4 * HEAD) == 0 else HEAD

    def gather(pick, sources, dst_of):
        def go(i, carry):
            cols = pl.ds(pl.multiple_of(i * step_cols, step_cols), step_cols)
            for kv in range(len(sources)):
                rows_got = jnp.dot(pick, sources[kv](cols), preferred_element_type=jnp.float32)
                dst_of(kv, cols, rows_got.astype(jnp.bfloat16))
            return carry

        lax.fori_loop(0, width // step_cols, go, 0)

    def part(c):
        return c // 2, pl.ds((c % 2) * half, half)

    def near_copy(c):
        kv, r = part(c)
        return remote((k_ref, v_ref)[kv].at[r], near.at[kv, r], s_near.at[c], r_near.at[c], twin)

    def cross_copy(c):
        kv, r = part(c)
        return remote(
            (k_ref, v_ref)[kv].at[r], big.at[0, kv, r], s_full.at[0, c], r_big.at[0, c], d + s
        )

    def twin_copy(c):
        kv, r = part(c)
        return remote(near.at[kv, r], big.at[1, kv, r], s_full.at[1, c], r_big.at[1, c], d + s)

    def relay_copy(c):
        kv, r = part(c)
        return remote(big.at[1, kv, r], big.at[0, kv, r], s_relay.at[c], r_big.at[0, c], relay_to)

    def fwd_copy(c):
        kv, r = part(c)
        return remote(big.at[0, kv, r], forwarded.at[kv, r], s_fwd.at[c], r_fwd.at[c], twin)

    def big_wait(slot, c):
        kv, r = part(c)
        remote(big.at[slot, kv, r], big.at[slot, kv, r], s_relay.at[c], r_big.at[slot, c], twin).wait_recv()

    def far_copy(i):
        r = pl.ds(far_start[i], far_rows[i])
        return remote(far_pack.at[:, r], far.at[:, r], s_far.at[i], r_far.at[i], fars[i][0])

    def pack_copy(kv):
        return remote(relay_pack.at[kv], outer.at[kv], s_pack.at[kv], r_outer.at[kv], relay_to)

    def hop_copy():
        kv, r = part(CHUNKS - 1)
        return remote((k_ref, v_ref)[kv].at[r], hop, s_hop.at[0], r_hop, d - 4 * s)

    def hop_on_copy():
        kv, r = part(CHUNKS - 1)
        return remote(hop, big.at[0, kv, r], s_hop.at[1], r_big.at[0, CHUNKS - 1], d + 3 * s)

    for slot, p, ok in sends_list:
        @pl.when(ok)
        def _(slot=slot, p=p):
            pick_copy(slot, p).start()

    for c in range(CHUNKS):
        near_copy(c).start()

    @pl.when(gate)
    def _():
        cross_copy(0).start()

    @pl.when(gets_relay)
    def _():
        hop_copy().start()

    for slot, p, ok in has_list:
        @pl.when(ok)
        def _(slot=slot, p=p):
            pick_copy(slot, p).wait_recv()
            if slot < 4:
                r = pl.ds(far_start[slot], far_rows[slot])

                def put(kv, cols, x):
                    far_pack[kv, r, cols] = x

                gather(got_far[r, :], (lambda c: k_ref[:, c], lambda c: v_ref[:, c]), put)
                far_copy(slot).start()

    @pl.when(gate)
    def _():
        for c in range(CHUNKS):
            near_copy(c).wait_recv()
        twin_copy(0).start()
        cross_copy(1).start()
        twin_copy(1).start()
        cross_copy(2).start()
        cross_copy(3).start()
        twin_copy(2).start()
        twin_copy(3).start()

    def as_bias(seen):
        return jnp.where(seen, 0.0, MASKED).astype(jnp.float32)

    def full_bias(side):
        block = lax.broadcasted_iota(jnp.int32, (1, rows), 1) // bs
        seen = jnp.zeros((1, rows), jnp.int32)
        for j in range(nblk):
            hit = (block == lists[0, 0, side, j]) & (jnp.full((1, rows), j) < counts[0, 0, side])
            seen = seen + hit.astype(jnp.int32)
        return as_bias(seen > 0)

    def listed_bias(side):
        column = lax.broadcasted_iota(jnp.int32, (1, cap1 * bs), 1)
        return as_bias(column < counts[0, 1, side] * bs)

    def wide(x, n):
        k = n // HEAD
        whole = jnp.concatenate([x] * k, axis=1) if k > 1 else x
        if n % HEAD:
            whole = jnp.concatenate([x] * (k + 1), axis=1)[:, :n]
        return whole

    def folded(p):
        n = p.shape[1]
        total = p[:, :HEAD]
        for i in range(1, n // HEAD):
            total = total + p[:, i * HEAD:(i + 1) * HEAD]
        return total

    def attend(keys, values, bias, first=False):
        def one(h):
            cols = pl.ds(pl.multiple_of(h * HEAD, HEAD), HEAD)
            sc = lax.dot_general(
                q_ref[:, cols], keys(cols), (((1,), (1,)), ((), ())),
                preferred_element_type=jnp.float32,
            ) * rate
            if bias is not None:
                sc = sc + bias
            n = sc.shape[1]
            best = jnp.broadcast_to(jnp.max(sc, axis=1, keepdims=True), (rows, HEAD))
            if not first:
                old = top[h]
                best = jnp.maximum(old, best)
            p = jnp.exp2(sc - wide(best, n))
            mixed = jnp.dot(
                p.astype(jnp.bfloat16), values(cols), preferred_element_type=jnp.float32
            )
            part_sum = folded(p)
            if first:
                tot[h] = part_sum
                acc[h] = mixed
            else:
                factor = jnp.exp2(old - best)
                tot[h] = tot[h] * factor + part_sum
                acc[h] = acc[h] * factor + mixed
            top[h] = best

        def step(i, carry):
            one(2 * i)
            one(2 * i + 1)
            return carry

        if heads % 2:
            lax.fori_loop(0, heads, lambda i, c: (one(i), c)[1], 0)
        else:
            lax.fori_loop(0, heads // 2, step, 0)

    def put_inner(kv, cols, x):
        inner[kv, :, cols] = x

    def put_outer(kv, cols, x):
        outer[kv, :, cols] = x

    attend(lambda c: k_ref[:, c], lambda c: v_ref[:, c], None, first=True)

    @pl.when(outermost & has_in)
    def _():
        hop_copy().wait_recv()
        hop_on_copy().start()

    @pl.when(outermost)
    def _():
        for c in range(CHUNKS):
            near_copy(c).wait_recv()

    attend(
        lambda c: near[0, :, c], lambda c: near[1, :, c],
        full_bias(jnp.where(gate, side_out, side_in)),
    )

    def pass_cross(c):
        big_wait(0, c)
        fwd_copy(c).start()

    def pass_twin(c):
        big_wait(1, c)

        @pl.when(has_in)
        def _():
            relay_copy(c).start()

    def pass_listed(kv):
        @pl.when(has_in)
        def _():
            def put_relay(_, cols, x):
                relay_pack[kv, :, cols] = x

            gather(got_near[...], (lambda c: big[0, kv, :, c],), put_relay)
            pack_copy(kv).start()

    @pl.when(gate)
    def _():
        pass_twin(0)
        pass_cross(0)
        pass_cross(1)
        pass_listed(0)
        pass_twin(1)

    arrives = [fars[1], fars[0], fars[3], fars[2]]
    for i in range(4):
        @pl.when(arrives[i][1])
        def _(i=i):
            far_copy(i).wait_recv()

        @pl.when(jnp.logical_not(arrives[i][1]))
        def _(i=i):
            for kv in range(2):
                far[kv, pl.ds(far_start[i], far_rows[i]), :] = jnp.zeros(
                    (far_rows[i], width), far.dtype
                )

    spare = (-sum(far_rows)) % HEAD
    if spare:
        for kv in range(2):
            far[kv, pl.ds(sum(far_rows), spare), :] = jnp.zeros((spare, width), far.dtype)
    column = lax.broadcasted_iota(jnp.int32, (1, sum(far_rows) + spare), 1)
    limit = jnp.zeros(column.shape, jnp.int32)
    for i in range(4):
        end = far_start[i] + counts[0, 2 + i // 2, i % 2] * bs
        limit = jnp.where(column >= far_start[i], end, limit)
    limit = jnp.where(column >= sum(far_rows), 0, limit)
    far_bias = as_bias(column < limit)
    attend(lambda c: far[0, :, c], lambda c: far[1, :, c], far_bias)

    def attend_inner():
        attend(lambda c: inner[0, :, c], lambda c: inner[1, :, c], listed_bias(side_in))

    def attend_big():
        attend(
            lambda c: big[0, 0, :, c], lambda c: big[0, 1, :, c],
            full_bias(jnp.where(gate, side_in, side_out)),
        )

    def attend_outer():
        attend(lambda c: outer[0, :, c], lambda c: outer[1, :, c], listed_bias(side_out))

    @pl.when(gate)
    def _():
        pass_cross(2)
        pass_cross(3)
        pass_listed(1)
        attend_big()
        pass_twin(2)
        big_wait(1, 3)
        gather(pick_near[side_in], (lambda c: big[1, 0, :, c], lambda c: big[1, 1, :, c]), put_inner)
        attend_inner()

        @pl.when(has_out)
        def _():
            for c in range(CHUNKS):
                fwd_copy(c).wait_recv()
            gather(
                pick_near[side_out],
                (lambda c: forwarded[0, :, c], lambda c: forwarded[1, :, c]), put_outer,
            )
            attend_outer()

    @pl.when(outermost)
    def _():
        @pl.when(has_out)
        def _():
            for c in (0, 1, 3):
                pass_cross(c)

        for c in range(CHUNKS):
            fwd_copy(c).wait_recv()
        gather(
            pick_near[side_in],
            (lambda c: forwarded[0, :, c], lambda c: forwarded[1, :, c]), put_inner,
        )
        attend_inner()

        @pl.when(has_out)
        def _():
            pass_cross(2)
            for kv in range(2):
                pack_copy(kv).wait_recv()
            attend_outer()
            attend_big()

    def finish(h, carry):
        cols = pl.ds(pl.multiple_of(h * HEAD, HEAD), HEAD)
        total = jnp.sum(tot[h], axis=1, keepdims=True)
        out_ref[:, cols] = (acc[h] / total).astype(out_ref.dtype)
        return carry

    lax.fori_loop(0, heads, finish, 0)

    for slot, p, ok in sends_list:
        @pl.when(ok)
        def _(slot=slot, p=p):
            pick_copy(slot, p).wait_send()
    for c in range(CHUNKS):
        near_copy(c).wait_send()

    @pl.when(gate)
    def _():
        for c in range(CHUNKS):
            cross_copy(c).wait_send()
            twin_copy(c).wait_send()

    for i, (p, ok) in enumerate(fars):
        @pl.when(ok)
        def _(i=i):
            far_copy(i).wait_send()

    @pl.when(relays)
    def _():
        for c in range(CHUNKS - 1):
            relay_copy(c).wait_send()
        for kv in range(2):
            pack_copy(kv).wait_send()

    @pl.when(gets_relay)
    def _():
        hop_copy().wait_send()

    @pl.when(outermost & has_in)
    def _():
        hop_on_copy().wait_send()

    @pl.when(forwards)
    def _():
        for c in range(CHUNKS):
            fwd_copy(c).wait_send()


def shards(n_ctx, queries, keys, values, kv_lists, kv_counts):
    rows, width = queries.shape
    heads = width // HEAD
    nblk = kv_lists.shape[3]
    bs = rows // nblk
    cap1 = nblk // 2
    far_rows = 2 * (nblk // 4 + nblk // 8) * bs
    far_room = far_rows + (-far_rows) % HEAD
    kv = jnp.bfloat16
    vmem = pl.BlockSpec(memory_space=pltpu.VMEM)
    smem = pl.BlockSpec(memory_space=pltpu.SMEM)
    dma = pltpu.SemaphoreType.DMA
    return pl.pallas_call(
        functools.partial(body, n_ctx, nblk),
        out_shape=jax.ShapeDtypeStruct((rows, width), jnp.bfloat16),
        in_specs=[vmem, vmem, vmem, smem, smem],
        out_specs=vmem,
        scratch_shapes=[
            pltpu.VMEM((2, rows, width), kv),
            pltpu.VMEM((2, rows, width), kv),
            pltpu.VMEM((2, 2, rows, width), kv),
            pltpu.VMEM((2, cap1 * bs, width), kv),
            pltpu.VMEM((2, cap1 * bs, width), kv),
            pltpu.VMEM((2, far_room, width), kv),
            pltpu.VMEM((2, far_rows, width), kv),
            pltpu.VMEM((2, cap1 * bs, width), kv),
            pltpu.VMEM((rows // 2, width), kv),
            pltpu.VMEM((2, cap1 * bs, rows), kv),
            pltpu.VMEM((far_rows, rows), kv),
            pltpu.VMEM((cap1 * bs, rows), kv),
            pltpu.VMEM((far_rows, rows), kv),
            pltpu.VMEM((heads, rows, HEAD), jnp.float32),
            pltpu.VMEM((heads, rows, HEAD), jnp.float32),
            pltpu.VMEM((heads, rows, HEAD), jnp.float32),
            dma((5,)), dma((CHUNKS,)), dma((2, CHUNKS)), dma((4,)), dma((CHUNKS,)), dma((CHUNKS,)), dma((2,)), dma((2,)),
            dma((5,)), dma((CHUNKS,)), dma((2, CHUNKS)), dma((4,)), dma((CHUNKS,)), dma((2,)), dma,
        ],
        compiler_params=pltpu.CompilerParams(
            collective_id=0, has_side_effects=True, vmem_limit_bytes=60 * 1024 * 1024
        ),
        name="radial",
    )(queries, keys, values, kv_lists, kv_counts)


def solution(mesh):
    in_specs = (
        P(("groups", "ctx"), None),
        P(("groups", "ctx"), None),
        P(("groups", "ctx"), None),
        P("ctx", None, None, None),
        P("ctx", None, None),
    )
    out_specs = P(("groups", "ctx"), None)
    return jax.shard_map(
        functools.partial(shards, mesh.shape["ctx"]),
        mesh=mesh, in_specs=in_specs, out_specs=out_specs, check_vma=False,
    )
```

```python
import functools
import math

import jax
import jax.numpy as jnp
from jax import lax
from jax.experimental import pallas as pl
from jax.experimental.pallas import tpu as pltpu
from jax.sharding import PartitionSpec as P

HEAD = 128
MASKED = -1e30
CHUNKS = 4
MESH = pl.DeviceIdType.MESH


def body(
    n_ctx, nblk,
    q_ref, k_ref, v_ref, lists, counts, out_ref,
    near, forwarded, big, inner, outer, far, far_pack, relay_pack, hop, pick_near, pick_far, got_near, got_far,
    acc, top, tot,
    s_list, s_near, s_full, s_far, s_relay, s_fwd, s_pack, s_hop,
    r_list, r_near, r_big, r_far, r_fwd, r_outer, r_hop,
):
    rows, width = q_ref.shape
    heads = width // HEAD
    bs = rows // nblk
    half = rows // 2
    cap1, cap2, cap3 = nblk // 2, nblk // 4, nblk // 8
    rate = math.log2(math.e) / math.sqrt(HEAD)

    d = lax.axis_index("ctx")
    place = lax.rem(d, 4)
    quad = d // 4
    quads = n_ctx // 4
    left = place < 2
    s = jnp.where(left, 1, -1)
    gate = (place == 1) | (place == 2)
    outermost = jnp.logical_not(gate)
    has_out = jnp.where(left, quad > 0, quad < quads - 1)
    has_in = jnp.where(left, quad < quads - 1, quad > 0)
    side_in = jnp.where(left, 1, 0)
    side_out = 1 - side_in
    twin = jnp.where(gate, d - s, d + s)
    relay_to = d + 3 * s
    relay_from = d - 3 * s
    relays = gate & has_in
    gets_relay = outermost & has_out
    forwards = gate | has_out
    fwd_arrives = outermost | has_out

    fars = []
    for distance in (4, 8):
        fars.append((d + distance, d + distance < n_ctx))
        fars.append((d - distance, d - distance >= 0))

    far_rows = (cap2 * bs, cap2 * bs, cap3 * bs, cap3 * bs)
    far_start = (0, cap2 * bs, 2 * cap2 * bs, (2 * cap2 + cap3) * bs)
    ahead = lax.broadcasted_iota(jnp.int32, (bs, rows), 1) - lax.broadcasted_iota(
        jnp.int32, (bs, rows), 0
    )

    def single_ones(level, side, j):
        hit = ahead == lists[0, level, side, j] * bs
        return jnp.where(hit, 1.0, 0.0).astype(jnp.bfloat16)

    for i in range(4):
        for j in range(far_rows[i] // bs):
            pick_far[pl.ds(far_start[i] + j * bs, bs), :] = single_ones(2 + i // 2, i % 2, j)
    for side in range(2):
        for j in range(cap1):
            pick_near[side, pl.ds(j * bs, bs), :] = single_ones(1, side, j)

    def to(device):
        return {"ctx": device}

    barrier = pltpu.get_barrier_semaphore()
    partners = [(p, ok) for p, ok in fars]
    always = jnp.bool_(True)
    partners += [
        (twin, always),
        (d + s, gate),
        (d + 3 * s, outermost),
        (relay_to, relays),
        (relay_from, gets_relay),
    ]
    count = jnp.int32(0)
    for p, ok in partners:
        count = count + ok.astype(jnp.int32)

        @pl.when(ok)
        def _(p=p):
            pl.semaphore_signal(barrier, inc=1, device_id=to(p), device_id_type=MESH)

    pl.semaphore_wait(barrier, count)

    def remote(src, dst, ssem, rsem, device):
        return pltpu.make_async_remote_copy(
            src_ref=src, dst_ref=dst, send_sem=ssem, recv_sem=rsem,
            device_id=to(device), device_id_type=MESH,
        )

    def pick_copy(i, device):
        if i == 4:
            return remote(pick_near.at[side_out], got_near, s_list.at[4], r_list.at[4], device)
        r = pl.ds(far_start[i], far_rows[i])
        return remote(pick_far.at[r], got_far.at[r], s_list.at[i], r_list.at[i], device)

    flip = (1, 0, 3, 2)
    sends_list = [(flip[i], p, ok) for i, (p, ok) in enumerate(fars)] + [(4, relay_from, gets_relay)]
    has_list = [(i, p, ok) for i, (p, ok) in enumerate(fars)] + [(4, relay_to, relays)]

    step_cols = 4 * HEAD if width % (4 * HEAD) == 0 else HEAD

    def gather(pick, sources, dst_of):
        def go(i, carry):
            cols = pl.ds(pl.multiple_of(i * step_cols, step_cols), step_cols)
            for kv in range(len(sources)):
                rows_got = jnp.dot(pick, sources[kv](cols), preferred_element_type=jnp.float32)
                dst_of(kv, cols, rows_got.astype(jnp.bfloat16))
            return carry

        lax.fori_loop(0, width // step_cols, go, 0)

    def part(c):
        return c // 2, pl.ds((c % 2) * half, half)

    def near_copy(c):
        kv, r = part(c)
        return remote((k_ref, v_ref)[kv].at[r], near.at[kv, r], s_near.at[c], r_near.at[c], twin)

    def cross_copy(c):
        kv, r = part(c)
        return remote(
            (k_ref, v_ref)[kv].at[r], big.at[0, kv, r], s_full.at[0, c], r_big.at[0, c], d + s
        )

    def twin_copy(c):
        kv, r = part(c)
        return remote(near.at[kv, r], big.at[1, kv, r], s_full.at[1, c], r_big.at[1, c], d + s)

    def relay_copy(c):
        kv, r = part(c)
        return remote(big.at[1, kv, r], big.at[0, kv, r], s_relay.at[c], r_big.at[0, c], relay_to)

    def fwd_copy(c):
        kv, r = part(c)
        return remote(big.at[0, kv, r], forwarded.at[kv, r], s_fwd.at[c], r_fwd.at[c], twin)

    def big_wait(slot, c):
        kv, r = part(c)
        remote(big.at[slot, kv, r], big.at[slot, kv, r], s_relay.at[c], r_big.at[slot, c], twin).wait_recv()

    def far_copy(i):
        r = pl.ds(far_start[i], far_rows[i])
        return remote(far_pack.at[:, r], far.at[:, r], s_far.at[i], r_far.at[i], fars[i][0])

    def pack_copy(kv):
        return remote(relay_pack.at[kv], outer.at[kv], s_pack.at[kv], r_outer.at[kv], relay_to)

    def hop_copy():
        kv, r = part(CHUNKS - 1)
        return remote((k_ref, v_ref)[kv].at[r], hop, s_hop.at[0], r_hop, d - 4 * s)

    def hop_on_copy():
        kv, r = part(CHUNKS - 1)
        return remote(hop, big.at[0, kv, r], s_hop.at[1], r_big.at[0, CHUNKS - 1], d + 3 * s)

    for slot, p, ok in sends_list:
        @pl.when(ok)
        def _(slot=slot, p=p):
            pick_copy(slot, p).start()

    for c in range(CHUNKS):
        near_copy(c).start()

    @pl.when(gate)
    def _():
        cross_copy(0).start()

    @pl.when(gets_relay)
    def _():
        hop_copy().start()

    for slot, p, ok in has_list:
        @pl.when(ok)
        def _(slot=slot, p=p):
            pick_copy(slot, p).wait_recv()
            if slot < 4:
                r = pl.ds(far_start[slot], far_rows[slot])

                def put(kv, cols, x):
                    far_pack[kv, r, cols] = x

                gather(got_far[r, :], (lambda c: k_ref[:, c], lambda c: v_ref[:, c]), put)
                far_copy(slot).start()

    @pl.when(gate)
    def _():
        for c in range(CHUNKS):
            near_copy(c).wait_recv()
        twin_copy(0).start()
        cross_copy(1).start()
        twin_copy(1).start()
        cross_copy(2).start()
        cross_copy(3).start()
        twin_copy(2).start()
        twin_copy(3).start()

    def as_bias(seen):
        return jnp.where(seen, 0.0, MASKED).astype(jnp.float32)

    def full_bias(side):
        block = lax.broadcasted_iota(jnp.int32, (1, rows), 1) // bs
        seen = jnp.zeros((1, rows), jnp.int32)
        for j in range(nblk):
            hit = (block == lists[0, 0, side, j]) & (jnp.full((1, rows), j) < counts[0, 0, side])
            seen = seen + hit.astype(jnp.int32)
        return as_bias(seen > 0)

    def listed_bias(side):
        column = lax.broadcasted_iota(jnp.int32, (1, cap1 * bs), 1)
        return as_bias(column < counts[0, 1, side] * bs)

    def wide(x, n):
        k = n // HEAD
        whole = jnp.concatenate([x] * k, axis=1) if k > 1 else x
        if n % HEAD:
            whole = jnp.concatenate([x] * (k + 1), axis=1)[:, :n]
        return whole

    def folded(p):
        n = p.shape[1]
        total = p[:, :HEAD]
        for i in range(1, n // HEAD):
            total = total + p[:, i * HEAD:(i + 1) * HEAD]
        return total

    together = max(n for n in (1, 2, 3, 4, 5) if heads % n == 0)

    def by_heads(one):
        def step(i, carry):
            for u in range(together):
                one(together * i + u)
            return carry

        lax.fori_loop(0, heads // together, step, 0)

    def attend(keys, values, bias, first=False):
        def one(h):
            cols = pl.ds(pl.multiple_of(h * HEAD, HEAD), HEAD)
            sc = lax.dot_general(
                q_ref[:, cols], keys(cols), (((1,), (1,)), ((), ())),
                preferred_element_type=jnp.float32,
            ) * rate
            if bias is not None:
                sc = sc + bias
            n = sc.shape[1]
            best = jnp.broadcast_to(jnp.max(sc, axis=1, keepdims=True), (rows, HEAD))
            if not first:
                old = top[h]
                best = jnp.maximum(old, best)
            p = jnp.exp2(sc - wide(best, n))
            mixed = jnp.dot(
                p.astype(jnp.bfloat16), values(cols), preferred_element_type=jnp.float32
            )
            part_sum = folded(p)
            if first:
                tot[h] = part_sum
                acc[h] = mixed
            else:
                factor = jnp.exp2(old - best)
                tot[h] = tot[h] * factor + part_sum
                acc[h] = acc[h] * factor + mixed
            top[h] = best

        by_heads(one)

    def put_inner(kv, cols, x):
        inner[kv, :, cols] = x

    def put_outer(kv, cols, x):
        outer[kv, :, cols] = x

    attend(lambda c: k_ref[:, c], lambda c: v_ref[:, c], None, first=True)

    @pl.when(outermost & has_in)
    def _():
        hop_copy().wait_recv()
        hop_on_copy().start()

    @pl.when(outermost)
    def _():
        for c in range(CHUNKS):
            near_copy(c).wait_recv()

    attend(
        lambda c: near[0, :, c], lambda c: near[1, :, c],
        full_bias(jnp.where(gate, side_out, side_in)),
    )

    def pass_cross(c):
        big_wait(0, c)
        fwd_copy(c).start()

    def pass_twin(c):
        big_wait(1, c)

        @pl.when(has_in)
        def _():
            relay_copy(c).start()

    def pass_listed(kv):
        @pl.when(has_in)
        def _():
            def put_relay(_, cols, x):
                relay_pack[kv, :, cols] = x

            gather(got_near[...], (lambda c: big[0, kv, :, c],), put_relay)
            pack_copy(kv).start()

    @pl.when(gate)
    def _():
        pass_twin(0)
        pass_cross(0)
        pass_cross(1)
        pass_listed(0)
        pass_twin(1)

    arrives = [fars[1], fars[0], fars[3], fars[2]]
    for i in range(4):
        @pl.when(arrives[i][1])
        def _(i=i):
            far_copy(i).wait_recv()

        @pl.when(jnp.logical_not(arrives[i][1]))
        def _(i=i):
            for kv in range(2):
                far[kv, pl.ds(far_start[i], far_rows[i]), :] = jnp.zeros(
                    (far_rows[i], width), far.dtype
                )

    spare = (-sum(far_rows)) % HEAD
    if spare:
        for kv in range(2):
            far[kv, pl.ds(sum(far_rows), spare), :] = jnp.zeros((spare, width), far.dtype)
    column = lax.broadcasted_iota(jnp.int32, (1, sum(far_rows) + spare), 1)
    limit = jnp.zeros(column.shape, jnp.int32)
    for i in range(4):
        end = far_start[i] + counts[0, 2 + i // 2, i % 2] * bs
        limit = jnp.where(column >= far_start[i], end, limit)
    limit = jnp.where(column >= sum(far_rows), 0, limit)
    far_bias = as_bias(column < limit)
    attend(lambda c: far[0, :, c], lambda c: far[1, :, c], far_bias)

    def attend_inner():
        attend(lambda c: inner[0, :, c], lambda c: inner[1, :, c], listed_bias(side_in))

    def attend_big():
        attend(
            lambda c: big[0, 0, :, c], lambda c: big[0, 1, :, c],
            full_bias(jnp.where(gate, side_in, side_out)),
        )

    def attend_outer():
        attend(lambda c: outer[0, :, c], lambda c: outer[1, :, c], listed_bias(side_out))

    @pl.when(gate)
    def _():
        pass_cross(2)
        pass_cross(3)
        pass_listed(1)
        attend_big()
        pass_twin(2)
        big_wait(1, 3)
        gather(pick_near[side_in], (lambda c: big[1, 0, :, c], lambda c: big[1, 1, :, c]), put_inner)
        attend_inner()

        @pl.when(has_out)
        def _():
            for c in range(CHUNKS):
                fwd_copy(c).wait_recv()
            gather(
                pick_near[side_out],
                (lambda c: forwarded[0, :, c], lambda c: forwarded[1, :, c]), put_outer,
            )
            attend_outer()

    @pl.when(outermost)
    def _():
        @pl.when(has_out)
        def _():
            for c in (0, 1, 3):
                pass_cross(c)

        for c in range(CHUNKS):
            fwd_copy(c).wait_recv()
        gather(
            pick_near[side_in],
            (lambda c: forwarded[0, :, c], lambda c: forwarded[1, :, c]), put_inner,
        )
        attend_inner()

        @pl.when(has_out)
        def _():
            for kv in range(2):
                pack_copy(kv).wait_recv()
            attend_outer()
            pass_cross(2)
            attend_big()

    def finish(h):
        cols = pl.ds(pl.multiple_of(h * HEAD, HEAD), HEAD)
        total = jnp.sum(tot[h], axis=1, keepdims=True)
        out_ref[:, cols] = (acc[h] / total).astype(out_ref.dtype)

    by_heads(finish)

    for slot, p, ok in sends_list:
        @pl.when(ok)
        def _(slot=slot, p=p):
            pick_copy(slot, p).wait_send()
    for c in range(CHUNKS):
        near_copy(c).wait_send()

    @pl.when(gate)
    def _():
        for c in range(CHUNKS):
            cross_copy(c).wait_send()
            twin_copy(c).wait_send()

    for i, (p, ok) in enumerate(fars):
        @pl.when(ok)
        def _(i=i):
            far_copy(i).wait_send()

    @pl.when(relays)
    def _():
        for c in range(CHUNKS - 1):
            relay_copy(c).wait_send()
        for kv in range(2):
            pack_copy(kv).wait_send()

    @pl.when(gets_relay)
    def _():
        hop_copy().wait_send()

    @pl.when(outermost & has_in)
    def _():
        hop_on_copy().wait_send()

    @pl.when(forwards)
    def _():
        for c in range(CHUNKS):
            fwd_copy(c).wait_send()


def shards(n_ctx, queries, keys, values, kv_lists, kv_counts):
    rows, width = queries.shape
    heads = width // HEAD
    nblk = kv_lists.shape[3]
    bs = rows // nblk
    cap1 = nblk // 2
    far_rows = 2 * (nblk // 4 + nblk // 8) * bs
    far_room = far_rows + (-far_rows) % HEAD
    kv = jnp.bfloat16
    vmem = pl.BlockSpec(memory_space=pltpu.VMEM)
    smem = pl.BlockSpec(memory_space=pltpu.SMEM)
    dma = pltpu.SemaphoreType.DMA
    return pl.pallas_call(
        functools.partial(body, n_ctx, nblk),
        out_shape=jax.ShapeDtypeStruct((rows, width), jnp.bfloat16),
        in_specs=[vmem, vmem, vmem, smem, smem],
        out_specs=vmem,
        scratch_shapes=[
            pltpu.VMEM((2, rows, width), kv),
            pltpu.VMEM((2, rows, width), kv),
            pltpu.VMEM((2, 2, rows, width), kv),
            pltpu.VMEM((2, cap1 * bs, width), kv),
            pltpu.VMEM((2, cap1 * bs, width), kv),
            pltpu.VMEM((2, far_room, width), kv),
            pltpu.VMEM((2, far_rows, width), kv),
            pltpu.VMEM((2, cap1 * bs, width), kv),
            pltpu.VMEM((rows // 2, width), kv),
            pltpu.VMEM((2, cap1 * bs, rows), kv),
            pltpu.VMEM((far_rows, rows), kv),
            pltpu.VMEM((cap1 * bs, rows), kv),
            pltpu.VMEM((far_rows, rows), kv),
            pltpu.VMEM((heads, rows, HEAD), jnp.float32),
            pltpu.VMEM((heads, rows, HEAD), jnp.float32),
            pltpu.VMEM((heads, rows, HEAD), jnp.float32),
            dma((5,)), dma((CHUNKS,)), dma((2, CHUNKS)), dma((4,)), dma((CHUNKS,)), dma((CHUNKS,)), dma((2,)), dma((2,)),
            dma((5,)), dma((CHUNKS,)), dma((2, CHUNKS)), dma((4,)), dma((CHUNKS,)), dma((2,)), dma,
        ],
        compiler_params=pltpu.CompilerParams(
            collective_id=0, has_side_effects=True, vmem_limit_bytes=60 * 1024 * 1024
        ),
        name="radial",
    )(queries, keys, values, kv_lists, kv_counts)


def solution(mesh):
    in_specs = (
        P(("groups", "ctx"), None),
        P(("groups", "ctx"), None),
        P(("groups", "ctx"), None),
        P("ctx", None, None, None),
        P("ctx", None, None),
    )
    out_specs = P(("groups", "ctx"), None)
    return jax.shard_map(
        functools.partial(shards, mesh.shape["ctx"]),
        mesh=mesh, in_specs=in_specs, out_specs=out_specs, check_vma=False,
    )
```

```python
import functools
import math

import jax
import jax.numpy as jnp
from jax import lax
from jax.experimental import pallas as pl
from jax.experimental.pallas import tpu as pltpu
from jax.sharding import PartitionSpec as P

HEAD = 128
MASKED = -1e30
CHUNKS = 4
MESH = pl.DeviceIdType.MESH


def body(
    n_ctx, nblk,
    q_hbm, k_hbm, v_hbm, lists, counts, out_ref,
    q_ref, k_ref, v_ref,
    near, forwarded, big, inner, outer, far, far_pack, relay_pack, hop, pick_near, pick_far, got_near, got_far,
    acc, top, tot,
    s_list, s_near, s_full, s_far, s_relay, s_fwd, s_pack, s_hop,
    r_list, r_near, r_big, r_far, r_fwd, r_outer, r_hop, r_own,
):
    own = [
        pltpu.make_async_copy(src, dst, r_own.at[i])
        for i, (src, dst) in enumerate(((k_hbm, k_ref), (v_hbm, v_ref), (q_hbm, q_ref)))
    ]
    for copy in own:
        copy.start()
    rows, width = q_ref.shape
    heads = width // HEAD
    bs = rows // nblk
    half = rows // 2
    cap1, cap2, cap3 = nblk // 2, nblk // 4, nblk // 8
    rate = math.log2(math.e) / math.sqrt(HEAD)

    d = lax.axis_index("ctx")
    place = lax.rem(d, 4)
    quad = d // 4
    quads = n_ctx // 4
    left = place < 2
    s = jnp.where(left, 1, -1)
    gate = (place == 1) | (place == 2)
    outermost = jnp.logical_not(gate)
    has_out = jnp.where(left, quad > 0, quad < quads - 1)
    has_in = jnp.where(left, quad < quads - 1, quad > 0)
    side_in = jnp.where(left, 1, 0)
    side_out = 1 - side_in
    twin = jnp.where(gate, d - s, d + s)
    relay_to = d + 3 * s
    relay_from = d - 3 * s
    relays = gate & has_in
    gets_relay = outermost & has_out
    forwards = gate | has_out
    fwd_arrives = outermost | has_out

    fars = []
    for distance in (4, 8):
        fars.append((d + distance, d + distance < n_ctx))
        fars.append((d - distance, d - distance >= 0))

    far_rows = (cap2 * bs, cap2 * bs, cap3 * bs, cap3 * bs)
    far_start = (0, cap2 * bs, 2 * cap2 * bs, (2 * cap2 + cap3) * bs)
    ahead = lax.broadcasted_iota(jnp.int32, (bs, rows), 1) - lax.broadcasted_iota(
        jnp.int32, (bs, rows), 0
    )

    def single_ones(level, side, j):
        hit = ahead == lists[0, level, side, j] * bs
        return jnp.where(hit, 1.0, 0.0).astype(jnp.bfloat16)

    for i in range(4):
        for j in range(far_rows[i] // bs):
            pick_far[pl.ds(far_start[i] + j * bs, bs), :] = single_ones(2 + i // 2, i % 2, j)
    for side in range(2):
        for j in range(cap1):
            pick_near[side, pl.ds(j * bs, bs), :] = single_ones(1, side, j)

    def to(device):
        return {"ctx": device}

    barrier = pltpu.get_barrier_semaphore()
    partners = [(p, ok) for p, ok in fars]
    always = jnp.bool_(True)
    partners += [
        (twin, always),
        (d + s, gate),
        (d + 3 * s, outermost),
        (relay_to, relays),
        (relay_from, gets_relay),
    ]
    count = jnp.int32(0)
    for p, ok in partners:
        count = count + ok.astype(jnp.int32)

        @pl.when(ok)
        def _(p=p):
            pl.semaphore_signal(barrier, inc=1, device_id=to(p), device_id_type=MESH)

    pl.semaphore_wait(barrier, count)

    def remote(src, dst, ssem, rsem, device):
        return pltpu.make_async_remote_copy(
            src_ref=src, dst_ref=dst, send_sem=ssem, recv_sem=rsem,
            device_id=to(device), device_id_type=MESH,
        )

    def pick_copy(i, device):
        if i == 4:
            return remote(pick_near.at[side_out], got_near, s_list.at[4], r_list.at[4], device)
        r = pl.ds(far_start[i], far_rows[i])
        return remote(pick_far.at[r], got_far.at[r], s_list.at[i], r_list.at[i], device)

    flip = (1, 0, 3, 2)
    sends_list = [(flip[i], p, ok) for i, (p, ok) in enumerate(fars)] + [(4, relay_from, gets_relay)]
    has_list = [(i, p, ok) for i, (p, ok) in enumerate(fars)] + [(4, relay_to, relays)]

    step_cols = 4 * HEAD if width % (4 * HEAD) == 0 else HEAD

    def gather(pick, sources, dst_of):
        def go(i, carry):
            cols = pl.ds(pl.multiple_of(i * step_cols, step_cols), step_cols)
            for kv in range(len(sources)):
                rows_got = jnp.dot(pick, sources[kv](cols), preferred_element_type=jnp.float32)
                dst_of(kv, cols, rows_got.astype(jnp.bfloat16))
            return carry

        lax.fori_loop(0, width // step_cols, go, 0)

    def part(c):
        return c // 2, pl.ds((c % 2) * half, half)

    def near_copy(c):
        kv, r = part(c)
        return remote((k_hbm, v_hbm)[kv].at[r], near.at[kv, r], s_near.at[c], r_near.at[c], twin)

    def cross_copy(c):
        kv, r = part(c)
        return remote(
            (k_hbm, v_hbm)[kv].at[r], big.at[0, kv, r], s_full.at[0, c], r_big.at[0, c], d + s
        )

    def twin_copy(c):
        kv, r = part(c)
        return remote(near.at[kv, r], big.at[1, kv, r], s_full.at[1, c], r_big.at[1, c], d + s)

    def relay_copy(c):
        kv, r = part(c)
        return remote(big.at[1, kv, r], big.at[0, kv, r], s_relay.at[c], r_big.at[0, c], relay_to)

    def fwd_copy(c):
        kv, r = part(c)
        return remote(big.at[0, kv, r], forwarded.at[kv, r], s_fwd.at[c], r_fwd.at[c], twin)

    def big_wait(slot, c):
        kv, r = part(c)
        remote(big.at[slot, kv, r], big.at[slot, kv, r], s_relay.at[c], r_big.at[slot, c], twin).wait_recv()

    def far_copy(i):
        r = pl.ds(far_start[i], far_rows[i])
        return remote(far_pack.at[:, r], far.at[:, r], s_far.at[i], r_far.at[i], fars[i][0])

    def pack_copy(kv):
        return remote(relay_pack.at[kv], outer.at[kv], s_pack.at[kv], r_outer.at[kv], relay_to)

    def hop_copy():
        kv, r = part(CHUNKS - 1)
        return remote((k_hbm, v_hbm)[kv].at[r], hop, s_hop.at[0], r_hop, d - 4 * s)

    def hop_on_copy():
        kv, r = part(CHUNKS - 1)
        return remote(hop, big.at[0, kv, r], s_hop.at[1], r_big.at[0, CHUNKS - 1], d + 3 * s)

    for slot, p, ok in sends_list:
        @pl.when(ok)
        def _(slot=slot, p=p):
            pick_copy(slot, p).start()

    for c in range(CHUNKS):
        near_copy(c).start()

    @pl.when(gate)
    def _():
        cross_copy(0).start()

    @pl.when(gets_relay)
    def _():
        hop_copy().start()

    for copy in own:
        copy.wait()

    for slot, p, ok in has_list:
        @pl.when(ok)
        def _(slot=slot, p=p):
            pick_copy(slot, p).wait_recv()
            if slot < 4:
                r = pl.ds(far_start[slot], far_rows[slot])

                def put(kv, cols, x):
                    far_pack[kv, r, cols] = x

                gather(got_far[r, :], (lambda c: k_ref[:, c], lambda c: v_ref[:, c]), put)
                far_copy(slot).start()

    @pl.when(gate)
    def _():
        for c in range(CHUNKS):
            near_copy(c).wait_recv()
        twin_copy(0).start()
        cross_copy(1).start()
        twin_copy(1).start()
        cross_copy(2).start()
        cross_copy(3).start()
        twin_copy(2).start()
        twin_copy(3).start()

    def as_bias(seen):
        return jnp.where(seen, 0.0, MASKED).astype(jnp.float32)

    def full_bias(side):
        block = lax.broadcasted_iota(jnp.int32, (1, rows), 1) // bs
        seen = jnp.zeros((1, rows), jnp.int32)
        for j in range(nblk):
            hit = (block == lists[0, 0, side, j]) & (jnp.full((1, rows), j) < counts[0, side, 0])
            seen = seen + hit.astype(jnp.int32)
        return as_bias(seen > 0)

    def listed_bias(side):
        column = lax.broadcasted_iota(jnp.int32, (1, cap1 * bs), 1)
        return as_bias(column < counts[0, side, 1] * bs)

    def wide(x, n):
        k = n // HEAD
        whole = jnp.concatenate([x] * k, axis=1) if k > 1 else x
        if n % HEAD:
            whole = jnp.concatenate([x] * (k + 1), axis=1)[:, :n]
        return whole

    def folded(p):
        n = p.shape[1]
        total = p[:, :HEAD]
        for i in range(1, n // HEAD):
            total = total + p[:, i * HEAD:(i + 1) * HEAD]
        return total

    together = max(n for n in (1, 2, 3, 4, 5) if heads % n == 0)

    def by_heads(one):
        def step(i, carry):
            for u in range(together):
                one(together * i + u)
            return carry

        lax.fori_loop(0, heads // together, step, 0)

    def attend(keys, values, bias, first=False):
        def one(h):
            cols = pl.ds(pl.multiple_of(h * HEAD, HEAD), HEAD)
            sc = lax.dot_general(
                q_ref[:, cols], keys(cols), (((1,), (1,)), ((), ())),
                preferred_element_type=jnp.float32,
            ) * rate
            if bias is not None:
                sc = sc + bias
            n = sc.shape[1]
            best = jnp.broadcast_to(jnp.max(sc, axis=1, keepdims=True), (rows, HEAD))
            if not first:
                old = top[h]
                best = jnp.maximum(old, best)
            p = jnp.exp2(sc - wide(best, n))
            mixed = jnp.dot(
                p.astype(jnp.bfloat16), values(cols), preferred_element_type=jnp.float32
            )
            part_sum = folded(p)
            if first:
                tot[h] = part_sum
                acc[h] = mixed
            else:
                factor = jnp.exp2(old - best)
                tot[h] = tot[h] * factor + part_sum
                acc[h] = acc[h] * factor + mixed
            top[h] = best

        by_heads(one)

    def put_inner(kv, cols, x):
        inner[kv, :, cols] = x

    def put_outer(kv, cols, x):
        outer[kv, :, cols] = x

    attend(lambda c: k_ref[:, c], lambda c: v_ref[:, c], None, first=True)

    @pl.when(outermost & has_in)
    def _():
        hop_copy().wait_recv()
        hop_on_copy().start()

    @pl.when(outermost)
    def _():
        for c in range(CHUNKS):
            near_copy(c).wait_recv()

    attend(
        lambda c: near[0, :, c], lambda c: near[1, :, c],
        full_bias(jnp.where(gate, side_out, side_in)),
    )

    def pass_cross(c):
        big_wait(0, c)
        fwd_copy(c).start()

    def pass_twin(c):
        big_wait(1, c)

        @pl.when(has_in)
        def _():
            relay_copy(c).start()

    def pass_listed(kv):
        @pl.when(has_in)
        def _():
            def put_relay(_, cols, x):
                relay_pack[kv, :, cols] = x

            gather(got_near[...], (lambda c: big[0, kv, :, c],), put_relay)
            pack_copy(kv).start()

    @pl.when(gate)
    def _():
        pass_twin(0)
        pass_cross(0)
        pass_cross(1)
        pass_listed(0)
        pass_twin(1)

    arrives = [fars[1], fars[0], fars[3], fars[2]]
    for i in range(4):
        @pl.when(arrives[i][1])
        def _(i=i):
            far_copy(i).wait_recv()

        @pl.when(jnp.logical_not(arrives[i][1]))
        def _(i=i):
            for kv in range(2):
                far[kv, pl.ds(far_start[i], far_rows[i]), :] = jnp.zeros(
                    (far_rows[i], width), far.dtype
                )

    spare = (-sum(far_rows)) % HEAD
    if spare:
        for kv in range(2):
            far[kv, pl.ds(sum(far_rows), spare), :] = jnp.zeros((spare, width), far.dtype)
    column = lax.broadcasted_iota(jnp.int32, (1, sum(far_rows) + spare), 1)
    limit = jnp.zeros(column.shape, jnp.int32)
    for i in range(4):
        end = far_start[i] + counts[0, i % 2, 2 + i // 2] * bs
        limit = jnp.where(column >= far_start[i], end, limit)
    limit = jnp.where(column >= sum(far_rows), 0, limit)
    far_bias = as_bias(column < limit)
    attend(lambda c: far[0, :, c], lambda c: far[1, :, c], far_bias)

    def attend_inner():
        attend(lambda c: inner[0, :, c], lambda c: inner[1, :, c], listed_bias(side_in))

    def attend_big():
        attend(
            lambda c: big[0, 0, :, c], lambda c: big[0, 1, :, c],
            full_bias(jnp.where(gate, side_in, side_out)),
        )

    def attend_outer():
        attend(lambda c: outer[0, :, c], lambda c: outer[1, :, c], listed_bias(side_out))

    @pl.when(gate)
    def _():
        pass_cross(2)
        pass_cross(3)
        pass_listed(1)
        attend_big()
        pass_twin(2)
        big_wait(1, 3)
        gather(pick_near[side_in], (lambda c: big[1, 0, :, c], lambda c: big[1, 1, :, c]), put_inner)
        attend_inner()

        @pl.when(has_out)
        def _():
            for c in range(CHUNKS):
                fwd_copy(c).wait_recv()
            gather(
                pick_near[side_out],
                (lambda c: forwarded[0, :, c], lambda c: forwarded[1, :, c]), put_outer,
            )
            attend_outer()

    @pl.when(outermost)
    def _():
        @pl.when(has_out)
        def _():
            for c in (0, 1, 3):
                pass_cross(c)

        for c in range(CHUNKS):
            fwd_copy(c).wait_recv()
        gather(
            pick_near[side_in],
            (lambda c: forwarded[0, :, c], lambda c: forwarded[1, :, c]), put_inner,
        )
        attend_inner()

        @pl.when(has_out)
        def _():
            for kv in range(2):
                pack_copy(kv).wait_recv()
            attend_outer()
            pass_cross(2)
            attend_big()

    def finish(h):
        cols = pl.ds(pl.multiple_of(h * HEAD, HEAD), HEAD)
        total = jnp.sum(tot[h], axis=1, keepdims=True)
        out_ref[:, cols] = (acc[h] / total).astype(out_ref.dtype)

    by_heads(finish)

    for slot, p, ok in sends_list:
        @pl.when(ok)
        def _(slot=slot, p=p):
            pick_copy(slot, p).wait_send()
    for c in range(CHUNKS):
        near_copy(c).wait_send()

    @pl.when(gate)
    def _():
        for c in range(CHUNKS):
            cross_copy(c).wait_send()
            twin_copy(c).wait_send()

    for i, (p, ok) in enumerate(fars):
        @pl.when(ok)
        def _(i=i):
            far_copy(i).wait_send()

    @pl.when(relays)
    def _():
        for c in range(CHUNKS - 1):
            relay_copy(c).wait_send()
        for kv in range(2):
            pack_copy(kv).wait_send()

    @pl.when(gets_relay)
    def _():
        hop_copy().wait_send()

    @pl.when(outermost & has_in)
    def _():
        hop_on_copy().wait_send()

    @pl.when(forwards)
    def _():
        for c in range(CHUNKS):
            fwd_copy(c).wait_send()


def shards(n_ctx, queries, keys, values, kv_lists, kv_counts):
    rows, width = queries.shape
    heads = width // HEAD
    nblk = kv_lists.shape[3]
    bs = rows // nblk
    cap1 = nblk // 2
    far_rows = 2 * (nblk // 4 + nblk // 8) * bs
    far_room = far_rows + (-far_rows) % HEAD
    kv = jnp.bfloat16
    vmem = pl.BlockSpec(memory_space=pltpu.VMEM)
    hbm = pl.BlockSpec(memory_space=pl.ANY)
    smem = pl.BlockSpec(memory_space=pltpu.SMEM)
    dma = pltpu.SemaphoreType.DMA
    return pl.pallas_call(
        functools.partial(body, n_ctx, nblk),
        out_shape=jax.ShapeDtypeStruct((rows, width), jnp.bfloat16),
        in_specs=[hbm, hbm, hbm, smem, smem],
        out_specs=vmem,
        scratch_shapes=[
            pltpu.VMEM((rows, width), kv),
            pltpu.VMEM((rows, width), kv),
            pltpu.VMEM((rows, width), kv),
            pltpu.VMEM((2, rows, width), kv),
            pltpu.VMEM((2, rows, width), kv),
            pltpu.VMEM((2, 2, rows, width), kv),
            pltpu.VMEM((2, cap1 * bs, width), kv),
            pltpu.VMEM((2, cap1 * bs, width), kv),
            pltpu.VMEM((2, far_room, width), kv),
            pltpu.VMEM((2, far_rows, width), kv),
            pltpu.VMEM((2, cap1 * bs, width), kv),
            pltpu.VMEM((rows // 2, width), kv),
            pltpu.VMEM((2, cap1 * bs, rows), kv),
            pltpu.VMEM((far_rows, rows), kv),
            pltpu.VMEM((cap1 * bs, rows), kv),
            pltpu.VMEM((far_rows, rows), kv),
            pltpu.VMEM((heads, rows, HEAD), jnp.float32),
            pltpu.VMEM((heads, rows, HEAD), jnp.float32),
            pltpu.VMEM((heads, rows, HEAD), jnp.float32),
            dma((5,)), dma((CHUNKS,)), dma((2, CHUNKS)), dma((4,)), dma((CHUNKS,)), dma((CHUNKS,)), dma((2,)), dma((2,)),
            dma((5,)), dma((CHUNKS,)), dma((2, CHUNKS)), dma((4,)), dma((CHUNKS,)), dma((2,)), dma, dma((3,)),
        ],
        compiler_params=pltpu.CompilerParams(
            collective_id=0, has_side_effects=True, vmem_limit_bytes=60 * 1024 * 1024
        ),
        name="radial",
    )(queries, keys, values, kv_lists, jnp.swapaxes(kv_counts, 1, 2))


def solution(mesh):
    in_specs = (
        P(("groups", "ctx"), None),
        P(("groups", "ctx"), None),
        P(("groups", "ctx"), None),
        P("ctx", None, None, None),
        P("ctx", None, None),
    )
    out_specs = P(("groups", "ctx"), None)
    return jax.shard_map(
        functools.partial(shards, mesh.shape["ctx"]),
        mesh=mesh, in_specs=in_specs, out_specs=out_specs, check_vma=False,
    )
```
